32 devices in a mesh: videos: 2 (over x), rows: 16 (over z, y, core).
Axes of the slice: x: 2, y: 2, z: 4, core: 2. Of those that a mesh axis runs over, the one named last changes fastest.
Arguments:
- latents: bfloat16 [4, 32, 64, 384], P('videos', 'rows'), parts along dimension 0, may hold values from -6 to 6
- conv_cache: bfloat16 [4, 32, 64, 384], P('videos', 'rows'), parts along dimension 0, may hold values from -4 to 4
- norm_gain: float32 [384], replicated, may hold values from 0.1 to 1.9
- conv_weight: bfloat16 [3, 3, 3, 384, 384], replicated, may hold values from -0.0625 to 0.0625
- attn_gain: float32 [384], replicated, may hold values from 0.1 to 1.9
- query_weight: bfloat16 [384, 384], replicated, may hold values from -3 to 3
- key_weight: bfloat16 [384, 384], replicated, may hold values from -3 to 3
- value_weight: bfloat16 [384, 384], replicated, may hold values from -0.3125 to 0.3125
- out_weight: bfloat16 [384, 384], replicated, may hold values from -0.3125 to 0.3125
- up_weight: bfloat16 [3, 3, 384, 192], replicated, may hold values from -0.109375 to 0.109375
Outputs:
- decoded: bfloat16 [4, 64, 128, 192], P('videos', 'rows'), parts along dimension 0
- next_cache: bfloat16 [4, 32, 64, 384], P('videos', 'rows'), parts along dimension 0
The draws below stay inside these ranges and needn't reach their ends.
There are 2 independent parts, one for each index of `videos`. The reference program is written for one: setup_inputs(seed, part) draws one part's arguments, and reference() takes and returns one part's arrays. A program takes and returns all parts, laid end to end along the dimension named above; an argument that names none is the same for every part. Nothing has to cross between parts.
All inputs are finite; a program needn't handle non-finite values.
Results may differ from the reference program's by a relative error of at most 0.0058.
Values may be sent and summed in bfloat16 or wider, within the bound.
A program may use at most 128 MiB of HBM per device.

```python
import math
import jax
import jax.numpy as jnp
from jax import lax

C = 384
C_HALF = 192
FRAMES = 2
CACHE = 2
WIDTH = 64
HEIGHT = 32


def own_noise(key, label, factor):
    noise = jnp.clip(jax.random.normal(jax.random.fold_in(key, label), (C, C), jnp.float32), -4.0, 4.0)
    return factor * noise / math.sqrt(C)


def draw_query_weight(key, part):
    mixed = own_noise(key, 201, 1.25)
    return jnp.clip(mixed, -3.0, 3.0).astype(jnp.bfloat16)


def draw_key_weight(key, part):
    mixed = own_noise(key, 202, 1.25)
    return jnp.clip(mixed, -3.0, 3.0).astype(jnp.bfloat16)


def levels(stream_key, shape, pieces, smallest, high):
    loudness = 1.0
    for dim, blocks in pieces:
        steps = jax.random.uniform(jax.random.fold_in(jax.random.fold_in(stream_key, 6), dim), (blocks,), jnp.float32, smallest / len(pieces), high / len(pieces))
        loudness = loudness * jnp.repeat(jnp.exp(steps), shape[dim] // blocks).reshape((-1,) + (1,) * (len(shape) - 1 - dim))
    return loudness


def normal_values(stream_key, shape, spread, most, split=(), dtype=jnp.bfloat16):
    loudness = levels(stream_key, shape, split, -0.22, 0.18) if split else 1.0
    drawn = jax.random.normal(stream_key, shape, jnp.float32) * spread * loudness
    return jnp.minimum(jnp.maximum(drawn, -most), most).astype(dtype)


def setup_inputs(seed: int = 0, part: int = 0) -> dict:
    splits = jax.random.split(jax.random.key(seed), 11)
    own_keys = jax.random.split(jax.random.fold_in(splits[10], part), 11)
    return {
        "latents": normal_values(own_keys[0], (FRAMES, HEIGHT, WIDTH, C), 1.0, 6.0, ((1, 16),)),
        "conv_cache": normal_values(own_keys[1], (CACHE, HEIGHT, WIDTH, C), 0.6, 4.0, ((1, 16),)),
        "norm_gain": jnp.clip(1.0 + 0.18 * jax.random.normal(splits[2], (C,), jnp.float32), 0.1, 1.9),
        "conv_weight": normal_values(splits[3], (3, 3, 3, C, C), (27 * C) ** -0.5, 0.0625),
        "attn_gain": jnp.clip(1.0 + 0.18 * jax.random.normal(splits[4], (C,), jnp.float32), 0.1, 1.9),
        "query_weight": draw_query_weight(jax.random.fold_in(splits[10], 71), part),
        "key_weight": draw_key_weight(jax.random.fold_in(splits[10], 71), part),
        "value_weight": normal_values(splits[7], (C, C), C ** -0.5, 0.3125),
        "out_weight": normal_values(splits[8], (C, C), C ** -0.5, 0.3125),
        "up_weight": normal_values(splits[9], (3, 3, C, C_HALF), (9 * C) ** -0.5, 0.109375),
    }


def normalize(values, gain):
    return values * lax.rsqrt(lax.optimization_barrier(jnp.mean(values * values, axis=-1, keepdims=True)) + 1e-06) * gain

def frame_attention(operands):
    query_rows, key_rows, value_rows = operands
    scores = jnp.dot(query_rows, key_rows.T, preferred_element_type=jnp.float32) * C ** (-0.5)
    largest = lax.optimization_barrier(jnp.max(scores, axis=-1, keepdims=True))
    weights = jnp.exp(scores - largest)
    totals = lax.optimization_barrier(jnp.sum(weights, axis=-1, keepdims=True))
    summed = jnp.dot(weights.astype(jnp.bfloat16), value_rows, preferred_element_type=jnp.float32)
    return (summed / totals).astype(jnp.bfloat16)

def reference(latents, conv_cache, norm_gain, conv_weight, attn_gain, query_weight, key_weight, value_weight, out_weight, up_weight):
    frames, height, width, channels = latents.shape
    values_in = latents.astype(jnp.float32)
    conv_input = jax.nn.silu(normalize(values_in, norm_gain)).astype(jnp.bfloat16)
    stacked = jnp.concatenate([conv_cache, conv_input], axis=0)
    padded = jnp.pad(stacked, ((0, 0), (1, 1), (1, 1), (0, 0)))
    total = jnp.zeros((frames * height * width, channels), jnp.float32)
    for tap_time in range(3):
        for tap_row in range(3):
            for tap_col in range(3):
                window = padded[tap_time:tap_time + frames, tap_row:tap_row + height, tap_col:tap_col + width]
                total = total + jnp.dot(window.reshape(-1, channels), conv_weight[tap_time, tap_row, tap_col], preferred_element_type=jnp.float32)
    resid = values_in + total.reshape(frames, height, width, channels)
    normed = normalize(resid, attn_gain).astype(jnp.bfloat16).reshape(-1, channels)
    queries = jnp.dot(normed, query_weight, preferred_element_type=jnp.float32).astype(jnp.bfloat16).reshape(frames, height * width, channels)
    keys = jnp.dot(normed, key_weight, preferred_element_type=jnp.float32).astype(jnp.bfloat16).reshape(frames, height * width, channels)
    values = jnp.dot(normed, value_weight, preferred_element_type=jnp.float32).astype(jnp.bfloat16).reshape(frames, height * width, channels)
    attended = lax.map(frame_attention, (queries, keys, values))
    projected = jnp.dot(attended.reshape(-1, channels), out_weight, preferred_element_type=jnp.float32)
    mid = (resid + projected.reshape(frames, height, width, channels)).astype(jnp.bfloat16)
    upsampled = jnp.repeat(jnp.repeat(mid, 2, axis=1), 2, axis=2)
    fine_pad = jnp.pad(upsampled, ((0, 0), (1, 1), (1, 1), (0, 0)))
    outputs = up_weight.shape[3]
    result = jnp.zeros((frames * 2 * height * 2 * width, outputs), jnp.float32)
    for tap_row in range(3):
        for tap_col in range(3):
            window = fine_pad[:, tap_row:tap_row + 2 * height, tap_col:tap_col + 2 * width]
            result = result + jnp.dot(window.reshape(-1, channels), up_weight[tap_row, tap_col], preferred_element_type=jnp.float32)
    decoded = result.reshape(frames, 2 * height, 2 * width, outputs).astype(jnp.bfloat16)
    next_cache = conv_input[frames - CACHE:]
    return (decoded, next_cache)
```

```python
import functools

import jax
import jax.numpy as jnp
from jax import lax
from jax.experimental import pallas as pl
from jax.experimental.pallas import tpu as pltpu
from jax.sharding import PartitionSpec as P

F32, BF16 = jnp.float32, jnp.bfloat16


def normalize(values, gain):
    return values * lax.rsqrt(jnp.mean(values * values, axis=-1, keepdims=True) + 1e-06) * gain


def with_columns(flat, width):
    values = flat.astype(F32)
    n = values.shape[0]
    column = lax.rem(lax.broadcasted_iota(jnp.int32, values.shape, 0), width)
    left = jnp.where(column == 0, 0.0, pltpu.roll(values, 1, 0)).astype(BF16)
    right = jnp.where(column == width - 1, 0.0, pltpu.roll(values, n - 1, 0)).astype(BF16)
    return jnp.concatenate([left, flat, right], axis=-1)


def dot_nt(a, b):
    return lax.dot_general(a, b, (((1,), (1,)), ((), ())), preferred_element_type=F32)


def dot(a, b):
    return jnp.dot(a, b, preferred_element_type=F32)


def kernel(
    nz, ny,
    latents, cache, gain, attn_gain, conv_hbm, q_hbm, k_hbm, v_hbm, o_hbm, up_hbm,
    decoded, next_cache,
    conv_w, q_w, k_w, v_w, o_w, up_w, up_p,
    lat, stk, ext, ext3, resid, keys, query, top, total, acc, mid, midx, mid3,
    w_sem, a_send, a_recv, z_send, z_recv, y_send, y_recv, c_send, c_recv,
):
    _, rows, width, channels = latents.shape
    band = 2 * rows
    outputs = decoded.shape[3]
    me = lax.axis_index("rows")
    chip, core = me // 2, me % 2
    z, y = chip // ny, chip % ny
    chips = nz * ny
    sibling = me + 1 - 2 * core
    has_prev, has_next = chip > 0, chip < chips - 1

    weights = [
        pltpu.make_async_copy(conv_hbm.at[pl.ds(3 * i, 3)], conv_w.at[pl.ds(3 * i, 3)], w_sem.at[i])
        for i in range(3)
    ]
    for i, (source, target) in enumerate(
        ((q_hbm, q_w), (k_hbm, k_w), (v_hbm, v_w), (o_hbm, o_w), (up_hbm, up_w))
    ):
        weights.append(pltpu.make_async_copy(source, target, w_sem.at[3 + i]))
    for copy in weights:
        copy.start()

    barrier = pltpu.get_barrier_semaphore()

    def greet(device):
        pl.semaphore_signal(
            barrier, inc=1, device_id={"rows": device}, device_id_type=pl.DeviceIdType.MESH
        )

    greet(sibling)
    met = 1

    @pl.when(has_prev)
    def _():
        greet(2 * chip - 2)
        greet(2 * chip - 1)

    @pl.when(has_next)
    def _():
        greet(2 * chip + 2)
        greet(2 * chip + 3)

    met = met + 2 * has_prev.astype(jnp.int32) + 2 * has_next.astype(jnp.int32)
    if ny > 1:

        @pl.when(z > 0)
        def _():
            greet(me - 2 * ny)

        @pl.when(z < nz - 1)
        def _():
            greet(me + 2 * ny)

        met = met + (z > 0).astype(jnp.int32) + (z < nz - 1).astype(jnp.int32)

    def remote(source, target, send, recv, device):
        return pltpu.make_async_remote_copy(
            src_ref=source,
            dst_ref=target,
            send_sem=send,
            recv_sem=recv,
            device_id={"rows": device},
            device_id_type=pl.DeviceIdType.MESH,
        )

    values_in = latents[...].astype(F32)
    normal = normalize(values_in, gain[...].reshape(1, 1, 1, channels))
    conv_input = (normal / (1.0 + jnp.exp(-normal))).astype(BF16)
    next_cache[...] = conv_input
    stk[0:2] = cache[...]
    stk[2:4] = conv_input

    pl.semaphore_wait(barrier, met)

    def halo(group, first, count, slot, source_row, target_row, device, kind):
        return remote(
            stk.at[pl.ds(group + first, count), pl.ds(source_row, 1)],
            ext.at[pl.ds(first, count), pl.ds(target_row, 1)],
            a_send.at[slot],
            a_recv.at[kind],
            device,
        )

    other = 1 - core
    to_sibling = [
        remote(
            stk.at[pl.ds(other + first, count)],
            ext.at[pl.ds(first, count), pl.ds(1 + rows * core, rows)],
            a_send.at[slot],
            a_recv.at[slot],
            sibling,
        )
        for slot, (first, count) in enumerate(((0, 1), (1, 2)))
    ]
    to_sibling.append(
        remote(
            latents.at[other], lat.at[pl.ds(rows * core, rows)], a_send.at[2], a_recv.at[2], sibling
        )
    )
    up_halo, down_halo = [], []
    for step, (first, count) in enumerate(((0, 1), (1, 2))):
        for g in range(2):
            slot = 3 + 2 * step + g
            down_halo.append(
                halo(g, first, count, slot, rows - 1, 0, 2 * chip + 2 + g, 3 + step)
            )
            up_halo.append(halo(g, first, count, slot, 0, band + 1, 2 * chip - 2 + g, 5 + step))
    sends_down = (core == 1) & has_next
    sends_up = (core == 0) & has_prev

    @pl.when(sends_down)
    def _():
        for copy in down_halo:
            copy.start()

    @pl.when(sends_up)
    def _():
        for copy in up_halo:
            copy.start()

    for copy in to_sibling:
        copy.start()

    ext[:, pl.ds(1 + rows * core, rows)] = stk[pl.ds(core, 3)]
    lat[pl.ds(rows * core, rows)] = latents[core]
    edge = jnp.zeros((3, 1, width, channels), BF16)

    @pl.when(jnp.logical_not(has_prev))
    def _():
        ext[:, 0:1] = edge

    @pl.when(jnp.logical_not(has_next))
    def _():
        ext[:, band + 1 : band + 2] = edge

    def arrived(target, sem):
        remote(target, target, a_send.at[0], sem, sibling).wait_recv()

    conv_out = jnp.zeros((band * width, channels), F32)
    for i in range(3):
        if i < 2:
            first, count = ((0, 1), (1, 2))[i]
            arrived(ext.at[pl.ds(first, count), pl.ds(1 + rows * other, rows)], a_recv.at[i])

            @pl.when(has_prev)
            def _():
                arrived(ext.at[pl.ds(first, count), pl.ds(0, 1)], a_recv.at[3 + i])

            @pl.when(has_next)
            def _():
                arrived(ext.at[pl.ds(first, count), pl.ds(band + 1, 1)], a_recv.at[5 + i])

        flat = ext[i].reshape((band + 2) * width, channels)
        ext3[i] = with_columns(flat, width)
        weights[i].wait()
        for j in range(3):
            window = ext3[i, j * width : (j + band) * width]
            conv_out = conv_out + dot(window, conv_w[3 * i + j])

    arrived(lat.at[pl.ds(rows * other, rows)], a_recv.at[2])
    resid_now = lat[...].reshape(band * width, channels).astype(F32) + conv_out
    resid[...] = resid_now
    normed = normalize(resid_now, attn_gain[...]).astype(BF16)
    keys[chip] = normed

    def up(block):
        index = block * ny + y
        return remote(
            keys.at[index], keys.at[index], z_send.at[block], z_recv.at[block], me + 2 * ny
        )

    def down(block):
        index = block * ny + y
        return remote(
            keys.at[index], keys.at[index], z_send.at[nz + block], z_recv.at[block], me - 2 * ny
        )

    def across(block):
        index = block * ny + y
        return remote(
            keys.at[index],
            keys.at[index],
            y_send.at[block],
            y_recv.at[block],
            me + 2 * (1 - 2 * y),
        )

    @pl.when(z < nz - 1)
    def _():
        up(z).start()

    @pl.when(z > 0)
    def _():
        down(z).start()

    if ny > 1:
        across(z).start()

    for copy in weights[3:]:
        copy.wait()
    queries = dot(normed, q_w[...]).astype(BF16)
    query[...] = (dot_nt(queries, k_w[...]) * channels ** (-0.5)).astype(BF16)

    scores = dot_nt(query[...], normed)
    largest = jnp.max(scores, axis=-1, keepdims=True)
    part = jnp.exp(scores - largest)
    top[...] = largest
    total[...] = jnp.sum(part, axis=-1, keepdims=True)
    acc[...] = dot(part.astype(BF16), normed)

    taps = {(0, 0): (0,), (0, 1): (1, 2), (1, 0): (0, 1), (1, 1): (2,)}
    for a in range(2):
        for t in range(2):
            for l_sets in range(2):
                for u in range(2):
                    summed = None
                    for j in taps[a, t]:
                        for l in taps[l_sets, u]:
                            term = up_w[j, l].astype(F32)
                            summed = term if summed is None else summed + term
                    up_p[a, l_sets, t, u * channels : (u + 1) * channels] = summed.astype(BF16)

    def attend(index):
        block = keys[index]
        scores = dot_nt(query[...], block)
        before = top[...]
        largest = jnp.maximum(before, jnp.max(scores, axis=-1, keepdims=True))
        part = jnp.exp(scores - largest)
        fade = jnp.exp(before - largest)
        top[...] = largest
        total[...] = total[...] * fade + jnp.sum(part, axis=-1, keepdims=True)
        acc[...] = acc[...] * fade + dot(part.astype(BF16), block)

    def z_arrived(block):
        index = block * ny + y
        remote(keys.at[index], keys.at[index], z_send.at[0], z_recv.at[block], sibling).wait_recv()

    def y_arrived(block):
        index = block * ny + 1 - y
        remote(keys.at[index], keys.at[index], y_send.at[0], y_recv.at[block], sibling).wait_recv()

    def gather_step(d, carry):
        low, high = z - d, z + d

        @pl.when(low >= 0)
        def _():
            z_arrived(low)

            @pl.when(z < nz - 1)
            def _():
                up(low).start()

            if ny > 1:
                across(low).start()

        @pl.when(high < nz)
        def _():
            z_arrived(high)

            @pl.when(z > 0)
            def _():
                down(high).start()

            if ny > 1:
                across(high).start()

        @pl.when(low >= 0)
        def _():
            attend(low * ny + y)

        @pl.when(high < nz)
        def _():
            attend(high * ny + y)

        if ny > 1:

            @pl.when(low + 1 >= 0)
            def _():
                y_arrived(low + 1)
                attend((low + 1) * ny + 1 - y)

            @pl.when((high - 1 < nz) & (d > 1))
            def _():
                y_arrived(high - 1)
                attend((high - 1) * ny + 1 - y)

        return carry

    lax.fori_loop(1, nz + 1 if ny > 1 else nz, gather_step, 0)

    mixed = (acc[...] / total[...]).astype(BF16)
    attended = dot(mixed, v_w[...]).astype(BF16)
    mid_now = (resid[...] + dot(attended, o_w[...])).astype(BF16)
    mid[...] = mid_now.reshape(band, width, channels)

    near = rows + 1
    mid_sibling = remote(
        mid.at[pl.ds(other * (rows - 1), near)],
        midx.at[core, pl.ds(core, near)],
        c_send.at[0],
        c_recv.at[0],
        sibling,
    )
    mid_down = remote(
        mid.at[pl.ds(band - 1, 1)],
        midx.at[core, pl.ds(0, 1)],
        c_send.at[1],
        c_recv.at[1 + core],
        2 * chip + 2,
    )
    mid_up = remote(
        mid.at[pl.ds(0, 1)],
        midx.at[core, pl.ds(rows + 1, 1)],
        c_send.at[2],
        c_recv.at[1 + core],
        2 * chip - 1,
    )

    @pl.when(has_next)
    def _():
        mid_down.start()

    @pl.when(has_prev)
    def _():
        mid_up.start()

    mid_sibling.start()
    midx[core, pl.ds(1 - core, near)] = mid[pl.ds(core * (rows - 1), near)]
    has_halo = ((core == 0) & has_prev) | ((core == 1) & has_next)
    edge_row = (rows + 1) * core

    @pl.when(jnp.logical_not(has_halo))
    def _():
        midx[:, pl.ds(edge_row, 1)] = jnp.zeros((2, 1, width, channels), BF16)

    for copy in to_sibling:
        copy.wait_send()

    @pl.when(sends_down)
    def _():
        for copy in down_halo:
            copy.wait_send()

    @pl.when(sends_up)
    def _():
        for copy in up_halo:
            copy.wait_send()

    def sent(block, carry):
        @pl.when((block <= z) & (z < nz - 1))
        def _():
            up(block).wait_send()

        @pl.when((block >= z) & (z > 0))
        def _():
            down(block).wait_send()

        if ny > 1:
            across(block).wait_send()
        return carry

    lax.fori_loop(0, nz, sent, 0)

    target = midx.at[other, pl.ds(core, near)]
    remote(
        midx.at[other, pl.ds(1 - core, near)],
        midx.at[other, pl.ds(1 - core, near)],
        c_send.at[0],
        c_recv.at[0],
        sibling,
    ).wait_recv()

    @pl.when(has_halo)
    def _():
        for f in range(2):
            landed = midx.at[f, pl.ds(edge_row, 1)]
            remote(landed, landed, c_send.at[0], c_recv.at[1 + f], sibling).wait_recv()

    for f in range(2):
        mid3[f] = with_columns(midx[f].reshape((rows + 2) * width, channels), width)

    fine = 2 * width
    at_row = lax.broadcasted_iota(jnp.int32, (fine, fine), 0)
    at_col = lax.broadcasted_iota(jnp.int32, (fine, fine), 1)
    weave = (at_col == (at_row % 2) * width + at_row // 2).astype(F32).astype(BF16)
    for a in range(2):
        sides = []
        for b in range(2):
            result = None
            for t in range(2):
                window = mid3[
                    :, (a + t) * width : (a + t + rows) * width,
                    b * channels : (b + 2) * channels,
                ].reshape(2 * rows * width, 2 * channels)
                term = dot(window, up_p[a, b, t])
                result = term if result is None else result + term
            sides.append(result.astype(BF16).reshape(2, rows, width, outputs))
        for f in range(2):
            for r in range(rows):
                pair = jnp.concatenate([sides[0][f, r], sides[1][f, r]], axis=0)
                decoded[f, 2 * r + a] = dot(weave, pair).astype(BF16)

    mid_sibling.wait_send()

    @pl.when(has_next)
    def _():
        mid_down.wait_send()

    @pl.when(has_prev)
    def _():
        mid_up.wait_send()


def solution(mesh):
    ny = 4 // mesh.shape["videos"]
    nz = mesh.shape["rows"] // (2 * ny)

    def shards(
        latents, conv_cache, norm_gain, conv_weight, attn_gain,
        query_weight, key_weight, value_weight, out_weight, up_weight,
    ):
        frames, rows, width, channels = latents.shape
        outputs = up_weight.shape[3]
        band = 2 * rows
        vmem = pl.BlockSpec(memory_space=pltpu.VMEM)
        hbm = pl.BlockSpec(memory_space=pl.ANY)
        square = pltpu.VMEM((channels, channels), BF16)
        dma = pltpu.SemaphoreType.DMA
        return pl.pallas_call(
            functools.partial(kernel, nz, ny),
            out_shape=(
                jax.ShapeDtypeStruct((frames, 2 * rows, 2 * width, outputs), BF16),
                jax.ShapeDtypeStruct(latents.shape, BF16),
            ),
            in_specs=[vmem] * 4 + [hbm] * 6,
            out_specs=(vmem, vmem),
            scratch_shapes=[
                pltpu.VMEM((9, 3 * channels, channels), BF16),
                square, square, square, square,
                pltpu.VMEM((3, 3, channels, outputs), BF16),
                pltpu.VMEM((2, 2, 2, 2 * channels, outputs), BF16),
                pltpu.VMEM((band, width, channels), BF16),
                pltpu.VMEM((4, rows, width, channels), BF16),
                pltpu.VMEM((3, band + 2, width, channels), BF16),
                pltpu.VMEM((3, (band + 2) * width, 3 * channels), BF16),
                pltpu.VMEM((band * width, channels), F32),
                pltpu.VMEM((nz * ny, band * width, channels), BF16),
                pltpu.VMEM((band * width, channels), BF16),
                pltpu.VMEM((band * width, 1), F32),
                pltpu.VMEM((band * width, 1), F32),
                pltpu.VMEM((band * width, channels), F32),
                pltpu.VMEM((band, width, channels), BF16),
                pltpu.VMEM((2, rows + 2, width, channels), BF16),
                pltpu.VMEM((2, (rows + 2) * width, 3 * channels), BF16),
                dma((8,)), dma((7,)), dma((7,)),
                dma((2 * nz,)), dma((nz,)), dma((nz,)), dma((nz,)),
                dma((3,)), dma((3,)),
            ],
            compiler_params=pltpu.CompilerParams(
                collective_id=0, has_side_effects=True, vmem_limit_bytes=50 * 1024 * 1024
            ),
        )(
            latents, conv_cache,
            norm_gain.reshape(1, channels), attn_gain.reshape(1, channels),
            conv_weight.reshape(9, 3 * channels, channels),
            query_weight, key_weight, value_weight, out_weight, up_weight,
        )

    split = P("videos", "rows", None, None)
    return jax.shard_map(
        shards,
        mesh=mesh,
        in_specs=(split, split) + (P(),) * 8,
        out_specs=(split, split),
        check_vma=False,
    )
```

```python
import functools

import jax
import jax.numpy as jnp
from jax import lax
from jax.experimental import pallas as pl
from jax.experimental.pallas import tpu as pltpu
from jax.sharding import PartitionSpec as P

F32, BF16 = jnp.float32, jnp.bfloat16


def normalize(values, gain):
    return values * lax.rsqrt(jnp.mean(values * values, axis=-1, keepdims=True) + 1e-06) * gain


def with_columns(flat, width):
    values = flat.astype(F32)
    n = values.shape[0]
    column = lax.rem(lax.broadcasted_iota(jnp.int32, values.shape, 0), width)
    left = jnp.where(column == 0, 0.0, pltpu.roll(values, 1, 0)).astype(BF16)
    right = jnp.where(column == width - 1, 0.0, pltpu.roll(values, n - 1, 0)).astype(BF16)
    return jnp.concatenate([left, flat, right], axis=-1)


def dot_nt(a, b):
    return lax.dot_general(a, b, (((1,), (1,)), ((), ())), preferred_element_type=F32)


def dot(a, b):
    return jnp.dot(a, b, preferred_element_type=F32)


def kernel(
    nz, ny,
    latents_hbm, cache_hbm, gain, attn_gain, conv_hbm, q_hbm, k_hbm, v_hbm, o_hbm, up_hbm,
    decoded, next_cache,
    latents, wide, conv_w, q_w, k_w, v_w, o_w, up_w, up_p,
    lat, stk, ext, ext3, resid, keys, query, top, total, acc, mid, midx, mid3,
    w_sem, a_send, a_recv, z_send, z_recv, y_send, y_recv, c_send, c_recv,
):
    _, rows, width, channels = latents.shape
    band = 2 * rows
    outputs = decoded.shape[3]
    me = lax.axis_index("rows")
    chip, core = me // 2, me % 2
    z, y = chip // ny, chip % ny
    chips = nz * ny
    sibling = me + 1 - 2 * core
    has_prev, has_next = chip > 0, chip < chips - 1

    latents_in = pltpu.make_async_copy(latents_hbm, latents, w_sem.at[8])
    cache_in = pltpu.make_async_copy(cache_hbm, stk.at[pl.ds(0, 2)], w_sem.at[9])
    latents_in.start()
    cache_in.start()
    weights = [
        pltpu.make_async_copy(conv_hbm.at[pl.ds(3 * i, 3)], conv_w.at[pl.ds(3 * i, 3)], w_sem.at[i])
        for i in range(3)
    ]
    for i, (source, target) in enumerate(
        ((q_hbm, q_w), (k_hbm, k_w), (v_hbm, v_w), (o_hbm, o_w), (up_hbm, up_w))
    ):
        weights.append(pltpu.make_async_copy(source, target, w_sem.at[3 + i]))
    for copy in weights:
        copy.start()

    barrier = pltpu.get_barrier_semaphore()

    def greet(device):
        pl.semaphore_signal(
            barrier, inc=1, device_id={"rows": device}, device_id_type=pl.DeviceIdType.MESH
        )

    greet(sibling)
    met = 1

    @pl.when(has_prev)
    def _():
        greet(2 * chip - 2)
        greet(2 * chip - 1)

    @pl.when(has_next)
    def _():
        greet(2 * chip + 2)
        greet(2 * chip + 3)

    met = met + 2 * has_prev.astype(jnp.int32) + 2 * has_next.astype(jnp.int32)
    if ny > 1:

        @pl.when(z > 0)
        def _():
            greet(me - 2 * ny)

        @pl.when(z < nz - 1)
        def _():
            greet(me + 2 * ny)

        met = met + (z > 0).astype(jnp.int32) + (z < nz - 1).astype(jnp.int32)

    def remote(source, target, send, recv, device):
        return pltpu.make_async_remote_copy(
            src_ref=source,
            dst_ref=target,
            send_sem=send,
            recv_sem=recv,
            device_id={"rows": device},
            device_id_type=pl.DeviceIdType.MESH,
        )

    cache_in.wait()
    latents_in.wait()
    pl.semaphore_wait(barrier, met)

    def halo(group, first, count, slot, source_row, target_row, device, kind):
        return remote(
            stk.at[pl.ds(group + first, count), pl.ds(source_row, 1)],
            ext.at[pl.ds(first, count), pl.ds(target_row, 1)],
            a_send.at[slot],
            a_recv.at[kind],
            device,
        )

    other = 1 - core
    to_sibling = [
        remote(
            stk.at[pl.ds(other + first, count)],
            ext.at[pl.ds(first, count), pl.ds(1 + rows * core, rows)],
            a_send.at[slot],
            a_recv.at[slot],
            sibling,
        )
        for slot, (first, count) in enumerate(((0, 1), (1, 2)))
    ]
    to_sibling.append(
        remote(
            latents.at[other], lat.at[pl.ds(rows * core, rows)], a_send.at[2], a_recv.at[2], sibling
        )
    )
    up_halo, down_halo = [], []
    for step, (first, count) in enumerate(((0, 1), (1, 2))):
        for g in range(2):
            slot = 3 + 2 * step + g
            down_halo.append(
                halo(g, first, count, slot, rows - 1, 0, 2 * chip + 2 + g, 3 + step)
            )
            up_halo.append(halo(g, first, count, slot, 0, band + 1, 2 * chip - 2 + g, 5 + step))
    sends_down = (core == 1) & has_next
    sends_up = (core == 0) & has_prev

    def start_halos(step):
        @pl.when(sends_down)
        def _():
            for copy in down_halo[2 * step : 2 * step + 2]:
                copy.start()

        @pl.when(sends_up)
        def _():
            for copy in up_halo[2 * step : 2 * step + 2]:
                copy.start()

    start_halos(0)
    to_sibling[0].start()
    to_sibling[2].start()
    normal = normalize(latents[...].astype(F32), gain[...].reshape(1, 1, 1, channels))
    conv_input = (normal / (1.0 + jnp.exp(-normal))).astype(BF16)
    stk[2:4] = conv_input
    start_halos(1)
    to_sibling[1].start()
    wide[...] = conv_input.astype(F32)
    cache_out = pltpu.make_async_copy(wide, next_cache, w_sem.at[10])
    cache_out.start()

    ext[:, pl.ds(1 + rows * core, rows)] = stk[pl.ds(core, 3)]
    lat[pl.ds(rows * core, rows)] = latents[core]
    edge = jnp.zeros((3, 1, width, channels), BF16)

    @pl.when(jnp.logical_not(has_prev))
    def _():
        ext[:, 0:1] = edge

    @pl.when(jnp.logical_not(has_next))
    def _():
        ext[:, band + 1 : band + 2] = edge

    def arrived(target, sem):
        remote(target, target, a_send.at[0], sem, sibling).wait_recv()

    conv_out = jnp.zeros((band * width, channels), F32)
    for i in range(3):
        if i < 2:
            first, count = ((0, 1), (1, 2))[i]
            arrived(ext.at[pl.ds(first, count), pl.ds(1 + rows * other, rows)], a_recv.at[i])

            @pl.when(has_prev)
            def _():
                arrived(ext.at[pl.ds(first, count), pl.ds(0, 1)], a_recv.at[3 + i])

            @pl.when(has_next)
            def _():
                arrived(ext.at[pl.ds(first, count), pl.ds(band + 1, 1)], a_recv.at[5 + i])

        flat = ext[i].reshape((band + 2) * width, channels)
        ext3[i] = with_columns(flat, width)
        weights[i].wait()
        for j in range(3):
            window = ext3[i, j * width : (j + band) * width]
            conv_out = conv_out + dot(window, conv_w[3 * i + j])

    arrived(lat.at[pl.ds(rows * other, rows)], a_recv.at[2])
    resid_now = lat[...].reshape(band * width, channels).astype(F32) + conv_out
    resid[...] = resid_now
    normed = normalize(resid_now, attn_gain[...].reshape(1, channels)).astype(BF16)
    keys[chip] = normed

    def piece(index, row):
        return keys.at[index, pl.ds(row * width, width)]

    def up(block, row):
        part = piece(block * ny + y, row)
        return remote(part, part, z_send.at[block], z_recv.at[block, row], me + 2 * ny)

    def down(block, row):
        part = piece(block * ny + y, row)
        return remote(part, part, z_send.at[nz + block], z_recv.at[block, row], me - 2 * ny)

    def across(block, row):
        part = piece(block * ny + y, row)
        return remote(part, part, y_send.at[block], y_recv.at[block], me + 2 * (1 - 2 * y))

    for row in range(band):

        @pl.when(z < nz - 1)
        def _():
            up(z, row).start()

        @pl.when(z > 0)
        def _():
            down(z, row).start()

        if ny > 1:
            across(z, row).start()

    for copy in weights[3:]:
        copy.wait()
    queries = dot(normed, q_w[...]).astype(BF16)
    query[...] = (dot_nt(queries, k_w[...]) * channels ** (-0.5)).astype(BF16)

    scores = dot_nt(query[...], normed)
    largest = jnp.max(scores, axis=-1, keepdims=True)
    part = jnp.exp(scores - largest)
    top[...] = largest
    total[...] = jnp.sum(part, axis=-1, keepdims=True)
    acc[...] = dot(part.astype(BF16), normed)

    taps = {(0, 0): (0,), (0, 1): (1, 2), (1, 0): (0, 1), (1, 1): (2,)}
    for a in range(2):
        for t in range(2):
            for l_sets in range(2):
                for u in range(2):
                    summed = None
                    for j in taps[a, t]:
                        for l in taps[l_sets, u]:
                            term = up_w[j, l].astype(F32)
                            summed = term if summed is None else summed + term
                    up_p[a, l_sets, t, :, u * channels : (u + 1) * channels] = summed.astype(BF16)

    def attend(index):
        block = keys[index]
        scores = dot_nt(query[...], block)
        before = top[...]
        largest = jnp.maximum(before, jnp.max(scores, axis=-1, keepdims=True))
        part = jnp.exp(scores - largest)
        fade = jnp.exp(before - largest)
        top[...] = largest
        total[...] = total[...] * fade + jnp.sum(part, axis=-1, keepdims=True)
        acc[...] = acc[...] * fade + dot(part.astype(BF16), block)

    def z_arrived(block, row):
        part = piece(block * ny + y, row)
        remote(part, part, z_send.at[0], z_recv.at[block, row], sibling).wait_recv()

    def attend_z(block):
        @pl.when((block >= 0) & (block < nz))
        def _():
            attend(block * ny + y)

    def attend_y(block):
        if ny > 1:

            @pl.when((block >= 0) & (block < nz))
            def _():
                whole = keys.at[block * ny + 1 - y]
                remote(whole, whole, y_send.at[0], y_recv.at[block], sibling).wait_recv()
                attend(block * ny + 1 - y)

    def gather_step(d, carry):
        low, high = z - d, z + d
        late_low = jnp.where(d > 1, low + 1, -1)
        late_high = jnp.where(d > 1, high - 1, nz)
        across_low = jnp.where(d > 1, low + 2, -1)
        across_high = jnp.where(d > 2, high - 2, nz)
        for row in range(band):

            @pl.when(low >= 0)
            def _():
                z_arrived(low, row)

                @pl.when(z < nz - 1)
                def _():
                    up(low, row).start()

                if ny > 1:
                    across(low, row).start()

            @pl.when(high < nz)
            def _():
                z_arrived(high, row)

                @pl.when(z > 0)
                def _():
                    down(high, row).start()

                if ny > 1:
                    across(high, row).start()

            if row == 0:
                attend_z(late_low)
            elif row == 1:
                attend_z(late_high)
            elif row == 2:
                attend_y(across_low)
            else:
                attend_y(across_high)

        return carry

    lax.fori_loop(1, nz, gather_step, 0)
    attend_z(z - nz + 1)
    attend_z(z + nz - 1)
    attend_y(z - nz + 2)
    attend_y(jnp.where(nz > 2, z + nz - 2, nz))
    attend_y(z - nz + 1)
    attend_y(z + nz - 1)

    mixed = (acc[...] / total[...]).astype(BF16)
    attended = dot(mixed, v_w[...]).astype(BF16)
    mid_now = (resid[...] + dot(attended, o_w[...])).astype(BF16)
    mid[...] = mid_now.reshape(band, width, channels)

    near = rows + 1
    mid_sibling = remote(
        mid.at[pl.ds(other * (rows - 1), near)],
        midx.at[core, pl.ds(core, near)],
        c_send.at[0],
        c_recv.at[0],
        sibling,
    )
    mid_down = remote(
        mid.at[pl.ds(band - 1, 1)],
        midx.at[core, pl.ds(0, 1)],
        c_send.at[1],
        c_recv.at[1 + core],
        2 * chip + 2,
    )
    mid_up = remote(
        mid.at[pl.ds(0, 1)],
        midx.at[core, pl.ds(rows + 1, 1)],
        c_send.at[2],
        c_recv.at[1 + core],
        2 * chip - 1,
    )

    @pl.when(has_next)
    def _():
        mid_down.start()

    @pl.when(has_prev)
    def _():
        mid_up.start()

    mid_sibling.start()
    midx[core, pl.ds(1 - core, near)] = mid[pl.ds(core * (rows - 1), near)]
    has_halo = ((core == 0) & has_prev) | ((core == 1) & has_next)
    edge_row = (rows + 1) * core

    @pl.when(jnp.logical_not(has_halo))
    def _():
        midx[:, pl.ds(edge_row, 1)] = jnp.zeros((2, 1, width, channels), BF16)

    for copy in to_sibling:
        copy.wait_send()

    @pl.when(sends_down)
    def _():
        for copy in down_halo:
            copy.wait_send()

    @pl.when(sends_up)
    def _():
        for copy in up_halo:
            copy.wait_send()

    def sent(block, carry):
        whole = keys.at[block * ny + y]

        @pl.when((block <= z) & (z < nz - 1))
        def _():
            remote(whole, whole, z_send.at[block], z_recv.at[0, 0], sibling).wait_send()

        @pl.when((block >= z) & (z > 0))
        def _():
            remote(whole, whole, z_send.at[nz + block], z_recv.at[0, 0], sibling).wait_send()

        if ny > 1:
            remote(whole, whole, y_send.at[block], y_recv.at[0], sibling).wait_send()
        return carry

    lax.fori_loop(0, nz, sent, 0)

    remote(
        midx.at[other, pl.ds(1 - core, near)],
        midx.at[other, pl.ds(1 - core, near)],
        c_send.at[0],
        c_recv.at[0],
        sibling,
    ).wait_recv()

    @pl.when(has_halo)
    def _():
        for f in range(2):
            landed = midx.at[f, pl.ds(edge_row, 1)]
            remote(landed, landed, c_send.at[0], c_recv.at[1 + f], sibling).wait_recv()

    for f in range(2):
        mid3[f] = with_columns(midx[f].reshape((rows + 2) * width, channels), width)

    fine = 2 * width
    at_row = lax.broadcasted_iota(jnp.int32, (fine, fine), 0)
    at_col = lax.broadcasted_iota(jnp.int32, (fine, fine), 1)
    weave = (at_col == (at_row % 2) * width + at_row // 2).astype(F32).astype(BF16)
    for a in range(2):
        sides = []
        for b in range(2):
            result = None
            for t in range(2):
                window = mid3[
                    :, (a + t) * width : (a + t + rows) * width,
                    b * channels : (b + 2) * channels,
                ].reshape(2 * rows * width, 2 * channels)
                term = dot_nt(window, up_p[a, b, t])
                result = term if result is None else result + term
            sides.append(result.astype(BF16).reshape(2, rows, width, outputs))
        for f in range(2):
            for r in range(rows):
                pair = jnp.concatenate([sides[0][f, r], sides[1][f, r]], axis=0)
                decoded[f, 2 * r + a] = dot(weave, pair).astype(BF16)

    cache_out.wait()
    mid_sibling.wait_send()

    @pl.when(has_next)
    def _():
        mid_down.wait_send()

    @pl.when(has_prev)
    def _():
        mid_up.wait_send()


def solution(mesh):
    ny = 4 // mesh.shape["videos"]
    nz = mesh.shape["rows"] // (2 * ny)

    def shards(
        latents, conv_cache, norm_gain, conv_weight, attn_gain,
        query_weight, key_weight, value_weight, out_weight, up_weight,
    ):
        frames, rows, width, channels = latents.shape
        outputs = up_weight.shape[3]
        band = 2 * rows
        vmem = pl.BlockSpec(memory_space=pltpu.VMEM)
        hbm = pl.BlockSpec(memory_space=pltpu.HBM)
        square = pltpu.VMEM((channels, channels), BF16)
        dma = pltpu.SemaphoreType.DMA
        decoded, next_cache = pl.pallas_call(
            functools.partial(kernel, nz, ny),
            out_shape=(
                jax.ShapeDtypeStruct((frames, 2 * rows, 2 * width, outputs), BF16),
                jax.ShapeDtypeStruct(latents.shape, F32),
            ),
            in_specs=[hbm] * 2 + [vmem] * 2 + [hbm] * 6,
            out_specs=(vmem, hbm),
            scratch_shapes=[
                pltpu.VMEM(latents.shape, BF16),
                pltpu.VMEM(latents.shape, F32),
                pltpu.VMEM((9, 3 * channels, channels), BF16),
                square, square, square, square,
                pltpu.VMEM((3, 3, outputs, channels), BF16),
                pltpu.VMEM((2, 2, 2, outputs, 2 * channels), BF16),
                pltpu.VMEM((band, width, channels), BF16),
                pltpu.VMEM((4, rows, width, channels), BF16),
                pltpu.VMEM((3, band + 2, width, channels), BF16),
                pltpu.VMEM((3, (band + 2) * width, 3 * channels), BF16),
                pltpu.VMEM((band * width, channels), F32),
                pltpu.VMEM((nz * ny, band * width, channels), BF16),
                pltpu.VMEM((band * width, channels), BF16),
                pltpu.VMEM((band * width, 1), F32),
                pltpu.VMEM((band * width, 1), F32),
                pltpu.VMEM((band * width, channels), F32),
                pltpu.VMEM((band, width, channels), BF16),
                pltpu.VMEM((2, rows + 2, width, channels), BF16),
                pltpu.VMEM((2, (rows + 2) * width, 3 * channels), BF16),
                dma((11,)), dma((7,)), dma((7,)),
                dma((2 * nz,)), dma((nz, band)), dma((nz,)), dma((nz,)),
                dma((3,)), dma((3,)),
            ],
            compiler_params=pltpu.CompilerParams(
                collective_id=0, has_side_effects=True, vmem_limit_bytes=60 * 1024 * 1024
            ),
        )(
            latents, conv_cache,
            norm_gain, attn_gain,
            conv_weight.reshape(9, 3 * channels, channels),
            query_weight, key_weight, value_weight, out_weight, up_weight.swapaxes(2, 3),
        )
        return decoded, next_cache.astype(BF16)

    split = P("videos", "rows", None, None)
    return jax.shard_map(
        shards,
        mesh=mesh,
        in_specs=(split, split) + (P(),) * 8,
        out_specs=(split, split),
        check_vma=False,
    )
```

```python
import functools

import jax
import jax.numpy as jnp
from jax import lax
from jax.experimental import pallas as pl
from jax.experimental.pallas import tpu as pltpu
from jax.sharding import PartitionSpec as P

F32, BF16 = jnp.float32, jnp.bfloat16


def normalize(values, gain):
    return values * lax.rsqrt(jnp.mean(values * values, axis=-1, keepdims=True) + 1e-06) * gain


def with_columns(flat, width):
    values = flat.astype(F32)
    n = values.shape[0]
    column = lax.rem(lax.broadcasted_iota(jnp.int32, values.shape, 0), width)
    left = jnp.where(column == 0, 0.0, pltpu.roll(values, 1, 0)).astype(BF16)
    right = jnp.where(column == width - 1, 0.0, pltpu.roll(values, n - 1, 0)).astype(BF16)
    return jnp.concatenate([left, flat, right], axis=-1)


def dot_nt(a, b):
    return lax.dot_general(a, b, (((1,), (1,)), ((), ())), preferred_element_type=F32)


def dot(a, b):
    return jnp.dot(a, b, preferred_element_type=F32)


def kernel(
    nz, ny,
    latents_hbm, cache_hbm, gain, attn_gain, conv_hbm, q_hbm, k_hbm, v_hbm, o_hbm, up_hbm,
    decoded, next_cache,
    conv_w, q_w, k_w, v_w, o_w, up_w, up_p,
    stk, own, ext, ext3, resid, keys, query, top, total, acc, mid, midx, mid3,
    w_sem, a_send, a_recv, z_send, z_recv, y_send, y_recv, c_send, c_recv,
):
    _, rows, width, channels = latents_hbm.shape
    band = 2 * rows
    outputs = decoded.shape[2]
    me = lax.axis_index("rows")
    chip, core = me // 2, me % 2
    z, y = chip // ny, chip % ny
    chips = nz * ny
    sibling = me + 1 - 2 * core
    has_prev, has_next = chip > 0, chip < chips - 1

    latents_in = pltpu.make_async_copy(latents_hbm, stk.at[pl.ds(2, 2)], w_sem.at[8])
    cache_in = pltpu.make_async_copy(cache_hbm, stk.at[pl.ds(0, 2)], w_sem.at[9])
    latents_in.start()
    cache_in.start()
    weights = [
        pltpu.make_async_copy(conv_hbm.at[pl.ds(3 * i, 3)], conv_w.at[pl.ds(3 * i, 3)], w_sem.at[i])
        for i in range(3)
    ]
    for i, (source, target) in enumerate(
        ((q_hbm, q_w), (k_hbm, k_w), (v_hbm, v_w), (o_hbm, o_w), (up_hbm, up_w))
    ):
        weights.append(pltpu.make_async_copy(source, target, w_sem.at[3 + i]))
    for copy in weights:
        copy.start()

    barrier = pltpu.get_barrier_semaphore()

    def greet(device):
        pl.semaphore_signal(
            barrier, inc=1, device_id={"rows": device}, device_id_type=pl.DeviceIdType.MESH
        )

    greet(sibling)
    met = 1

    @pl.when(has_prev)
    def _():
        greet(2 * chip - 2)
        greet(2 * chip - 1)

    @pl.when(has_next)
    def _():
        greet(2 * chip + 2)
        greet(2 * chip + 3)

    met = met + 2 * has_prev.astype(jnp.int32) + 2 * has_next.astype(jnp.int32)
    if ny > 1:

        @pl.when(z > 0)
        def _():
            greet(me - 2 * ny)

        @pl.when(z < nz - 1)
        def _():
            greet(me + 2 * ny)

        met = met + (z > 0).astype(jnp.int32) + (z < nz - 1).astype(jnp.int32)

    def remote(source, target, send, recv, device):
        return pltpu.make_async_remote_copy(
            src_ref=source,
            dst_ref=target,
            send_sem=send,
            recv_sem=recv,
            device_id={"rows": device},
            device_id_type=pl.DeviceIdType.MESH,
        )

    cache_in.wait()
    latents_in.wait()
    pl.semaphore_wait(barrier, met)

    other = 1 - core
    pair = core
    third = 2 - 2 * core
    others_pair = other
    others_third = 2 - 2 * other
    mine = pl.ds(1 + rows * core, rows)
    siblings = pl.ds(1 + rows * other, rows)
    above, below = pl.ds(0, 1), pl.ds(band + 1, 1)
    to_sibling = [
        remote(
            stk.at[pl.ds(2 * other, 2)],
            ext.at[pl.ds(others_pair, 2), mine],
            a_send.at[0], a_recv.at[0], sibling,
        ),
        remote(
            stk.at[pl.ds(2 - other, 1)],
            ext.at[pl.ds(others_third, 1), mine],
            a_send.at[1], a_recv.at[1], sibling,
        ),
    ]
    down_halo = [
        remote(
            stk.at[pl.ds(2 * g, 2), pl.ds(rows - 1, 1)],
            ext.at[pl.ds(g, 2), above],
            a_send.at[2 + g], a_recv.at[2], 2 * chip + 2 + g,
        )
        for g in range(2)
    ]
    up_halo = [
        remote(
            stk.at[pl.ds(2 * g, 2), pl.ds(0, 1)],
            ext.at[pl.ds(g, 2), below],
            a_send.at[2 + g], a_recv.at[4], 2 * chip - 2 + g,
        )
        for g in range(2)
    ]
    pass_above, pass_below = [
        remote(
            ext.at[pl.ds(1, 1), row],
            ext.at[pl.ds(others_third, 1), row],
            a_send.at[4 + i], a_recv.at[3 + 2 * i], sibling,
        )
        for i, row in enumerate((above, below))
    ]
    sends_down = (core == 1) & has_next
    sends_up = (core == 0) & has_prev

    @pl.when(sends_down)
    def _():
        for copy in down_halo:
            copy.start()

    @pl.when(sends_up)
    def _():
        for copy in up_halo:
            copy.start()

    for copy in to_sibling:
        copy.start()

    ext[:, mine] = stk[pl.ds(core, 3)]
    edge = jnp.zeros((3, 1, width, channels), BF16)

    @pl.when(jnp.logical_not(has_prev))
    def _():
        ext[:, 0:1] = edge

    @pl.when(jnp.logical_not(has_next))
    def _():
        ext[:, band + 1 : band + 2] = edge

    def arrived(target, sem):
        remote(target, target, a_send.at[0], sem, sibling).wait_recv()

    def activate(values):
        normal = normalize(values.astype(F32), gain[...].reshape(1, channels))
        return (normal / (1.0 + jnp.exp(-normal))).astype(BF16)

    conv_out = jnp.zeros((band * width, channels), F32)
    for i in range(3):
        t = lax.rem(i + core, 3)
        if i == 0:

            @pl.when(has_prev)
            def _():
                arrived(ext.at[pl.ds(pair, 2), above], a_recv.at[2])
                pass_above.start()

            @pl.when(has_next)
            def _():
                arrived(ext.at[pl.ds(pair, 2), below], a_recv.at[4])
                pass_below.start()

            arrived(ext.at[pl.ds(pair, 2), siblings], a_recv.at[0])
        if i == 2:
            arrived(ext.at[pl.ds(third, 1), siblings], a_recv.at[1])

            @pl.when(has_prev)
            def _():
                arrived(ext.at[pl.ds(third, 1), above], a_recv.at[3])

            @pl.when(has_next)
            def _():
                arrived(ext.at[pl.ds(third, 1), below], a_recv.at[5])

        fresh = core == (0 if i == 2 else 1)

        @pl.when(fresh)
        def _():
            flat = ext[t].reshape((band + 2) * width, channels)
            ext3[i] = with_columns(activate(flat), width)

        @pl.when(jnp.logical_not(fresh))
        def _():
            ext3[i] = with_columns(ext[t].reshape((band + 2) * width, channels), width)

        pltpu.make_async_copy(
            conv_hbm.at[pl.ds(3 * t, 3)], conv_w.at[pl.ds(3 * t, 3)], w_sem.at[t]
        ).wait()
        for j in range(3):
            window = ext3[i, j * width : (j + band) * width]
            conv_out = conv_out + dot(window, conv_w[3 * t + j])

    resid_now = ext[2, 1 : 1 + band].reshape(band * width, channels).astype(F32) + conv_out
    resid[...] = resid_now
    normed = normalize(resid_now, attn_gain[...].reshape(1, channels)).astype(BF16)
    keys[chip] = normed

    def piece(index, row):
        return keys.at[index, pl.ds(row * width, width)]

    def up(block, row):
        part = piece(block * ny + y, row)
        return remote(part, part, z_send.at[block], z_recv.at[block, row], me + 2 * ny)

    def down(block, row):
        part = piece(block * ny + y, row)
        return remote(part, part, z_send.at[nz + block], z_recv.at[block, row], me - 2 * ny)

    def across(block, row):
        part = piece(block * ny + y, row)
        return remote(part, part, y_send.at[block], y_recv.at[block], me + 2 * (1 - 2 * y))

    for row in range(band):

        @pl.when(z < nz - 1)
        def _():
            up(z, row).start()

        @pl.when(z > 0)
        def _():
            down(z, row).start()

        if ny > 1:
            across(z, row).start()

    own[...] = activate(stk[2:4].reshape(2 * rows * width, channels)).reshape(own.shape)
    cache_out = pltpu.make_async_copy(own, next_cache, w_sem.at[10])
    cache_out.start()
    for copy in weights[3:]:
        copy.wait()
    queries = dot(normed, q_w[...]).astype(BF16)
    query[...] = (dot_nt(queries, k_w[...]) * channels ** (-0.5)).astype(BF16)

    scores = dot_nt(query[...], normed)
    largest = jnp.max(scores, axis=-1, keepdims=True)
    part = jnp.exp(scores - largest)
    top[...] = largest
    total[...] = jnp.sum(part, axis=-1, keepdims=True)
    acc[...] = dot(part.astype(BF16), normed)

    taps = {(0, 0): (0,), (0, 1): (1, 2), (1, 0): (0, 1), (1, 1): (2,)}
    for a in range(2):
        for t in range(2):
            for l_sets in range(2):
                for u in range(2):
                    summed = None
                    for j in taps[a, t]:
                        for l in taps[l_sets, u]:
                            term = up_w[j, l].astype(F32)
                            summed = term if summed is None else summed + term
                    up_p[a, l_sets, t, :, u * channels : (u + 1) * channels] = summed.astype(BF16)

    def attend(index):
        block = keys[index]
        scores = dot_nt(query[...], block)
        before = top[...]
        largest = jnp.maximum(before, jnp.max(scores, axis=-1, keepdims=True))
        part = jnp.exp(scores - largest)
        fade = jnp.exp(before - largest)
        top[...] = largest
        total[...] = total[...] * fade + jnp.sum(part, axis=-1, keepdims=True)
        acc[...] = acc[...] * fade + dot(part.astype(BF16), block)

    def z_arrived(block, row):
        part = piece(block * ny + y, row)
        remote(part, part, z_send.at[0], z_recv.at[block, row], sibling).wait_recv()

    def attend_z(block):
        @pl.when((block >= 0) & (block < nz))
        def _():
            attend(block * ny + y)

    def attend_y(block):
        if ny > 1:

            @pl.when((block >= 0) & (block < nz))
            def _():
                whole = keys.at[block * ny + 1 - y]
                remote(whole, whole, y_send.at[0], y_recv.at[block], sibling).wait_recv()
                attend(block * ny + 1 - y)

    def gather_step(d, carry):
        low, high = z - d, z + d
        late_low = jnp.where(d > 1, low + 1, -1)
        late_high = jnp.where(d > 1, high - 1, nz)
        across_low = jnp.where(d > 1, low + 2, -1)
        across_high = jnp.where(d > 2, high - 2, nz)
        for row in range(band):

            @pl.when(low >= 0)
            def _():
                z_arrived(low, row)

                @pl.when(z < nz - 1)
                def _():
                    up(low, row).start()

                if ny > 1:
                    across(low, row).start()

            @pl.when(high < nz)
            def _():
                z_arrived(high, row)

                @pl.when(z > 0)
                def _():
                    down(high, row).start()

                if ny > 1:
                    across(high, row).start()

            if row == 0:
                attend_z(late_low)
            elif row == 1:
                attend_z(late_high)
            elif row == 2:
                attend_y(across_low)
            else:
                attend_y(across_high)

        return carry

    lax.fori_loop(1, nz, gather_step, 0)
    attend_z(z - nz + 1)
    attend_z(z + nz - 1)
    attend_y(z - nz + 2)
    attend_y(jnp.where(nz > 2, z + nz - 2, nz))
    attend_y(z - nz + 1)
    attend_y(z + nz - 1)

    mixed = (acc[...] / total[...]).astype(BF16)
    attended = dot(mixed, v_w[...]).astype(BF16)
    mid_now = (resid[...] + dot(attended, o_w[...])).astype(BF16)
    mid[...] = mid_now.reshape(band, width, channels)

    near = rows + 1
    mid_sibling = remote(
        mid.at[pl.ds(other * (rows - 1), near)],
        midx.at[core, pl.ds(core, near)],
        c_send.at[0],
        c_recv.at[0],
        sibling,
    )
    mid_down = remote(
        mid.at[pl.ds(band - 1, 1)],
        midx.at[core, pl.ds(0, 1)],
        c_send.at[1],
        c_recv.at[1 + core],
        2 * chip + 2,
    )
    mid_up = remote(
        mid.at[pl.ds(0, 1)],
        midx.at[core, pl.ds(rows + 1, 1)],
        c_send.at[2],
        c_recv.at[1 + core],
        2 * chip - 1,
    )

    @pl.when(has_next)
    def _():
        mid_down.start()

    @pl.when(has_prev)
    def _():
        mid_up.start()

    mid_sibling.start()
    midx[core, pl.ds(1 - core, near)] = mid[pl.ds(core * (rows - 1), near)]
    has_halo = ((core == 0) & has_prev) | ((core == 1) & has_next)
    edge_row = (rows + 1) * core

    @pl.when(jnp.logical_not(has_halo))
    def _():
        midx[:, pl.ds(edge_row, 1)] = jnp.zeros((2, 1, width, channels), BF16)

    for copy in to_sibling:
        copy.wait_send()

    @pl.when(has_prev)
    def _():
        pass_above.wait_send()

    @pl.when(has_next)
    def _():
        pass_below.wait_send()

    @pl.when(sends_down)
    def _():
        for copy in down_halo:
            copy.wait_send()

    @pl.when(sends_up)
    def _():
        for copy in up_halo:
            copy.wait_send()

    def sent(block, carry):
        whole = keys.at[block * ny + y]

        @pl.when((block <= z) & (z < nz - 1))
        def _():
            remote(whole, whole, z_send.at[block], z_recv.at[0, 0], sibling).wait_send()

        @pl.when((block >= z) & (z > 0))
        def _():
            remote(whole, whole, z_send.at[nz + block], z_recv.at[0, 0], sibling).wait_send()

        if ny > 1:
            remote(whole, whole, y_send.at[block], y_recv.at[0], sibling).wait_send()
        return carry

    lax.fori_loop(0, nz, sent, 0)

    remote(
        midx.at[other, pl.ds(1 - core, near)],
        midx.at[other, pl.ds(1 - core, near)],
        c_send.at[0],
        c_recv.at[0],
        sibling,
    ).wait_recv()

    @pl.when(has_halo)
    def _():
        for f in range(2):
            landed = midx.at[f, pl.ds(edge_row, 1)]
            remote(landed, landed, c_send.at[0], c_recv.at[1 + f], sibling).wait_recv()

    for f in range(2):
        mid3[f] = with_columns(midx[f].reshape((rows + 2) * width, channels), width)

    fine = 2 * width
    at_row = lax.broadcasted_iota(jnp.int32, (fine, fine), 0)
    at_col = lax.broadcasted_iota(jnp.int32, (fine, fine), 1)
    weave = (at_col == (at_row % 2) * width + at_row // 2).astype(F32).astype(BF16)
    for a in range(2):
        sides = []
        for b in range(2):
            result = None
            for t in range(2):
                window = mid3[
                    :, (a + t) * width : (a + t + rows) * width,
                    b * channels : (b + 2) * channels,
                ].reshape(2 * rows * width, 2 * channels)
                term = dot_nt(window, up_p[a, b, t])
                result = term if result is None else result + term
            sides.append(result.astype(BF16).reshape(2, rows, width, outputs))
        for f in range(2):
            for r in range(rows):
                pair = jnp.concatenate([sides[0][f, r], sides[1][f, r]], axis=0)
                decoded[f, 2 * r + a] = lax.dot_general(
                    pair, weave, (((0,), (1,)), ((), ())), preferred_element_type=F32
                ).astype(BF16)

    cache_out.wait()
    mid_sibling.wait_send()

    @pl.when(has_next)
    def _():
        mid_down.wait_send()

    @pl.when(has_prev)
    def _():
        mid_up.wait_send()


def finish(decoded_in, cache_in, decoded, next_cache):
    decoded[...] = decoded_in[...]
    next_cache[...] = cache_in[...]


def solution(mesh):
    ny = 4 // mesh.shape["videos"]
    nz = mesh.shape["rows"] // (2 * ny)

    def shards(
        latents, conv_cache, norm_gain, conv_weight, attn_gain,
        query_weight, key_weight, value_weight, out_weight, up_weight,
    ):
        frames, rows, width, channels = latents.shape
        outputs = up_weight.shape[3]
        band = 2 * rows
        vmem = pl.BlockSpec(memory_space=pltpu.VMEM)
        hbm = pl.BlockSpec(memory_space=pltpu.HBM)
        square = pltpu.VMEM((channels, channels), BF16)
        dma = pltpu.SemaphoreType.DMA
        decoded, next_cache = pl.pallas_call(
            functools.partial(kernel, nz, ny),
            out_shape=(
                jax.ShapeDtypeStruct((frames, 2 * rows, outputs, 2 * width), BF16),
                jax.ShapeDtypeStruct(latents.shape, BF16),
            ),
            in_specs=[hbm] * 2 + [vmem] * 2 + [hbm] * 6,
            out_specs=(vmem, hbm),
            scratch_shapes=[
                pltpu.VMEM((9, 3 * channels, channels), BF16),
                square, square, square, square,
                pltpu.VMEM((3, 3, outputs, channels), BF16),
                pltpu.VMEM((2, 2, 2, outputs, 2 * channels), BF16),
                pltpu.VMEM((4, rows, width, channels), BF16),
                pltpu.VMEM(latents.shape, BF16),
                pltpu.VMEM((3, band + 2, width, channels), BF16),
                pltpu.VMEM((3, (band + 2) * width, 3 * channels), BF16),
                pltpu.VMEM((band * width, channels), F32),
                pltpu.VMEM((nz * ny, band * width, channels), BF16),
                pltpu.VMEM((band * width, channels), BF16),
                pltpu.VMEM((band * width, 1), F32),
                pltpu.VMEM((band * width, 1), F32),
                pltpu.VMEM((band * width, channels), F32),
                pltpu.VMEM((band, width, channels), BF16),
                pltpu.VMEM((2, rows + 2, width, channels), BF16),
                pltpu.VMEM((2, (rows + 2) * width, 3 * channels), BF16),
                dma((11,)), dma((6,)), dma((6,)),
                dma((2 * nz,)), dma((nz, band)), dma((nz,)), dma((nz,)),
                dma((3,)), dma((3,)),
            ],
            compiler_params=pltpu.CompilerParams(
                collective_id=0, has_side_effects=True, vmem_limit_bytes=60 * 1024 * 1024
            ),
        )(
            latents, conv_cache,
            norm_gain, attn_gain,
            conv_weight.reshape(9, 3 * channels, channels),
            query_weight, key_weight, value_weight, out_weight, up_weight.swapaxes(2, 3),
        )
        decoded, next_cache = pl.pallas_call(
            finish,
            out_shape=(
                jax.ShapeDtypeStruct(decoded.shape, BF16),
                jax.ShapeDtypeStruct(next_cache.shape, BF16),
            ),
            in_specs=[vmem] * 2,
            out_specs=(vmem, vmem),
        )(decoded, next_cache)
        return decoded.swapaxes(2, 3), next_cache

    split = P("videos", "rows", None, None)
    return jax.shard_map(
        shards,
        mesh=mesh,
        in_specs=(split, split) + (P(),) * 8,
        out_specs=(split, split),
        check_vma=False,
    )
```

```python
import functools

import jax
import jax.numpy as jnp
from jax import lax
from jax.experimental import pallas as pl
from jax.experimental.pallas import tpu as pltpu
from jax.sharding import PartitionSpec as P

F32, BF16 = jnp.float32, jnp.bfloat16


def normalize(values, gain):
    return values * lax.rsqrt(jnp.mean(values * values, axis=-1, keepdims=True) + 1e-06) * gain


def with_columns(flat, width):
    values = flat.astype(F32)
    n = values.shape[0]
    column = lax.rem(lax.broadcasted_iota(jnp.int32, values.shape, 0), width)
    left = jnp.where(column == 0, 0.0, pltpu.roll(values, 1, 0)).astype(BF16)
    right = jnp.where(column == width - 1, 0.0, pltpu.roll(values, n - 1, 0)).astype(BF16)
    return jnp.concatenate([left, flat, right], axis=-1)


def dot_nt(a, b):
    return lax.dot_general(a, b, (((1,), (1,)), ((), ())), preferred_element_type=F32)


def dot(a, b):
    return jnp.dot(a, b, preferred_element_type=F32)


def kernel(
    nz, ny,
    latents_hbm, cache_hbm, gain, attn_gain, conv_hbm, q_hbm, k_hbm, v_hbm, o_hbm, up_hbm,
    decoded, next_cache,
    conv_w, q_w, k_w, v_w, o_w, up_w, up_p,
    stk, own, ext, ext3, resid, keys, query, top, total, acc, mid, midx, mid3,
    w_sem, a_send, a_recv, z_send, z_recv, y_send, y_recv, c_send, c_recv,
):
    _, rows, width, channels = latents_hbm.shape
    band = 2 * rows
    outputs = decoded.shape[2]
    me = lax.axis_index("rows")
    chip, core = me // 2, me % 2
    z, y = chip // ny, chip % ny
    chips = nz * ny
    sibling = me + 1 - 2 * core
    has_prev, has_next = chip > 0, chip < chips - 1

    latents_in = pltpu.make_async_copy(latents_hbm, stk.at[pl.ds(2, 2)], w_sem.at[8])
    cache_in = pltpu.make_async_copy(cache_hbm, stk.at[pl.ds(0, 2)], w_sem.at[9])
    latents_in.start()
    cache_in.start()
    weights = [
        pltpu.make_async_copy(conv_hbm.at[pl.ds(3 * i, 3)], conv_w.at[pl.ds(3 * i, 3)], w_sem.at[i])
        for i in range(3)
    ]
    for i, (source, target) in enumerate(
        ((q_hbm, q_w), (k_hbm, k_w), (v_hbm, v_w), (o_hbm, o_w), (up_hbm, up_w))
    ):
        weights.append(pltpu.make_async_copy(source, target, w_sem.at[3 + i]))
    for copy in weights:
        copy.start()

    barrier = pltpu.get_barrier_semaphore()

    def greet(device):
        pl.semaphore_signal(
            barrier, inc=1, device_id={"rows": device}, device_id_type=pl.DeviceIdType.MESH
        )

    greet(sibling)
    met = 1

    @pl.when(has_prev)
    def _():
        greet(2 * chip - 2)
        greet(2 * chip - 1)

    @pl.when(has_next)
    def _():
        greet(2 * chip + 2)
        greet(2 * chip + 3)

    met = met + 2 * has_prev.astype(jnp.int32) + 2 * has_next.astype(jnp.int32)
    if ny > 1:

        @pl.when(z > 0)
        def _():
            greet(me - 2 * ny)

        @pl.when(z < nz - 1)
        def _():
            greet(me + 2 * ny)

        met = met + (z > 0).astype(jnp.int32) + (z < nz - 1).astype(jnp.int32)

    def remote(source, target, send, recv, device):
        return pltpu.make_async_remote_copy(
            src_ref=source,
            dst_ref=target,
            send_sem=send,
            recv_sem=recv,
            device_id={"rows": device},
            device_id_type=pl.DeviceIdType.MESH,
        )

    cache_in.wait()
    latents_in.wait()
    pl.semaphore_wait(barrier, met)

    other = 1 - core
    pair = core
    third = 2 - 2 * core
    others_pair = other
    others_third = 2 - 2 * other
    mine = pl.ds(1 + rows * core, rows)
    siblings = pl.ds(1 + rows * other, rows)
    above, below = pl.ds(0, 1), pl.ds(band + 1, 1)
    to_sibling = [
        remote(
            stk.at[pl.ds(2 * other, 2)],
            ext.at[pl.ds(others_pair, 2), mine],
            a_send.at[0], a_recv.at[0], sibling,
        ),
        remote(
            stk.at[pl.ds(2 - other, 1)],
            ext.at[pl.ds(others_third, 1), mine],
            a_send.at[1], a_recv.at[1], sibling,
        ),
    ]
    down_halo = [
        remote(
            stk.at[pl.ds(2 * g, 2), pl.ds(rows - 1, 1)],
            ext.at[pl.ds(g, 2), above],
            a_send.at[2 + g], a_recv.at[2], 2 * chip + 2 + g,
        )
        for g in range(2)
    ]
    up_halo = [
        remote(
            stk.at[pl.ds(2 * g, 2), pl.ds(0, 1)],
            ext.at[pl.ds(g, 2), below],
            a_send.at[2 + g], a_recv.at[4], 2 * chip - 2 + g,
        )
        for g in range(2)
    ]
    pass_above, pass_below = [
        remote(
            ext.at[pl.ds(1, 1), row],
            ext.at[pl.ds(others_third, 1), row],
            a_send.at[4 + i], a_recv.at[3 + 2 * i], sibling,
        )
        for i, row in enumerate((above, below))
    ]
    sends_down = (core == 1) & has_next
    sends_up = (core == 0) & has_prev

    @pl.when(sends_down)
    def _():
        for copy in down_halo:
            copy.start()

    @pl.when(sends_up)
    def _():
        for copy in up_halo:
            copy.start()

    for copy in to_sibling:
        copy.start()

    ext[:, mine] = stk[pl.ds(core, 3)]
    edge = jnp.zeros((3, 1, width, channels), BF16)

    @pl.when(jnp.logical_not(has_prev))
    def _():
        ext[:, 0:1] = edge

    @pl.when(jnp.logical_not(has_next))
    def _():
        ext[:, band + 1 : band + 2] = edge

    def arrived(target, sem):
        remote(target, target, a_send.at[0], sem, sibling).wait_recv()

    def activate(values):
        normal = normalize(values.astype(F32), gain[...].reshape(1, channels))
        return (normal / (1.0 + jnp.exp(-normal))).astype(BF16)

    conv_out = jnp.zeros((band * width, channels), F32)
    for i in range(3):
        t = lax.rem(i + core, 3)
        if i == 0:

            @pl.when(has_prev)
            def _():
                arrived(ext.at[pl.ds(pair, 2), above], a_recv.at[2])
                pass_above.start()

            @pl.when(has_next)
            def _():
                arrived(ext.at[pl.ds(pair, 2), below], a_recv.at[4])
                pass_below.start()

            arrived(ext.at[pl.ds(pair, 2), siblings], a_recv.at[0])
        if i == 2:
            arrived(ext.at[pl.ds(third, 1), siblings], a_recv.at[1])

            @pl.when(has_prev)
            def _():
                arrived(ext.at[pl.ds(third, 1), above], a_recv.at[3])

            @pl.when(has_next)
            def _():
                arrived(ext.at[pl.ds(third, 1), below], a_recv.at[5])

        fresh = core == (0 if i == 2 else 1)

        @pl.when(fresh)
        def _():
            flat = ext[t].reshape((band + 2) * width, channels)
            ext3[i] = with_columns(activate(flat), width)

        @pl.when(jnp.logical_not(fresh))
        def _():
            ext3[i] = with_columns(ext[t].reshape((band + 2) * width, channels), width)

        pltpu.make_async_copy(
            conv_hbm.at[pl.ds(3 * t, 3)], conv_w.at[pl.ds(3 * t, 3)], w_sem.at[t]
        ).wait()
        for j in range(3):
            window = ext3[i, j * width : (j + band) * width]
            conv_out = conv_out + dot(window, conv_w[3 * t + j])

    resid_now = ext[2, 1 : 1 + band].reshape(band * width, channels).astype(F32) + conv_out
    resid[...] = resid_now
    normed = normalize(resid_now, attn_gain[...].reshape(1, channels)).astype(BF16)
    keys[chip] = normed

    def piece(index, row):
        return keys.at[index, pl.ds(row * width, width)]

    def up(block, row):
        part = piece(block * ny + y, row)
        return remote(part, part, z_send.at[block], z_recv.at[block, row], me + 2 * ny)

    def down(block, row):
        part = piece(block * ny + y, row)
        return remote(part, part, z_send.at[nz + block], z_recv.at[block, row], me - 2 * ny)

    def across(block, row):
        part = piece(block * ny + y, row)
        return remote(part, part, y_send.at[block], y_recv.at[block], me + 2 * (1 - 2 * y))

    for row in range(band):

        @pl.when(z < nz - 1)
        def _():
            up(z, row).start()

        @pl.when(z > 0)
        def _():
            down(z, row).start()

        if ny > 1:
            across(z, row).start()

    for copy in weights[3:]:
        copy.wait()
    queries = dot(normed, q_w[...]).astype(BF16)
    query[...] = (dot_nt(queries, k_w[...]) * channels ** (-0.5)).astype(BF16)

    scores = dot_nt(query[...], normed)
    largest = jnp.max(scores, axis=-1, keepdims=True)
    part = jnp.exp(scores - largest)
    top[...] = largest
    total[...] = jnp.sum(part, axis=-1, keepdims=True)
    acc[...] = dot(part.astype(BF16), normed)

    taps = {(0, 0): (0,), (0, 1): (1, 2), (1, 0): (0, 1), (1, 1): (2,)}
    def add_taps(a, t):
        for side in range(2):
            for u in range(2):
                summed = None
                for j in taps[a, t]:
                    for l in taps[side, u]:
                        term = up_w[j, l].astype(F32)
                        summed = term if summed is None else summed + term
                up_p[a, side, t, :, u * channels : (u + 1) * channels] = summed.astype(BF16)

    def attend(index):
        block = keys[index]
        scores = dot_nt(query[...], block)
        before = top[...]
        largest = jnp.maximum(before, jnp.max(scores, axis=-1, keepdims=True))
        part = jnp.exp(scores - largest)
        fade = jnp.exp(before - largest)
        top[...] = largest
        total[...] = total[...] * fade + jnp.sum(part, axis=-1, keepdims=True)
        acc[...] = acc[...] * fade + dot(part.astype(BF16), block)

    def z_arrived(block, row):
        part = piece(block * ny + y, row)
        remote(part, part, z_send.at[0], z_recv.at[block, row], sibling).wait_recv()

    def attend_z(block):
        @pl.when((block >= 0) & (block < nz))
        def _():
            attend(block * ny + y)

    def attend_y(block):
        if ny > 1:

            @pl.when((block >= 0) & (block < nz))
            def _():
                whole = keys.at[block * ny + 1 - y]
                remote(whole, whole, y_send.at[0], y_recv.at[block], sibling).wait_recv()
                attend(block * ny + 1 - y)

    def gather_step(d, carry):
        low, high = z - d, z + d
        late_low = jnp.where(d > 1, low + 1, -1)
        late_high = jnp.where(d > 1, high - 1, nz)
        across_low = jnp.where(d > 1, low + 2, -1)
        across_high = jnp.where(d > 2, high - 2, nz)
        for row in range(band):

            @pl.when(low >= 0)
            def _():
                z_arrived(low, row)

                @pl.when(z < nz - 1)
                def _():
                    up(low, row).start()

                if ny > 1:
                    across(low, row).start()

            @pl.when(high < nz)
            def _():
                z_arrived(high, row)

                @pl.when(z > 0)
                def _():
                    down(high, row).start()

                if ny > 1:
                    across(high, row).start()

            if row == 0:
                attend_z(late_low)
            elif row == 1:
                attend_z(late_high)
            elif row == 2:
                attend_y(across_low)
            else:
                attend_y(across_high)
            if row < 4:

                @pl.when(d == 1)
                def _():
                    add_taps(row // 2, row % 2)

        return carry

    lax.fori_loop(1, nz, gather_step, 0)
    attend_z(z - nz + 1)
    attend_z(z + nz - 1)
    attend_y(z - nz + 2)
    attend_y(jnp.where(nz > 2, z + nz - 2, nz))
    attend_y(z - nz + 1)
    attend_y(z + nz - 1)

    mixed = (acc[...] / total[...]).astype(BF16)
    attended = dot(mixed, v_w[...]).astype(BF16)
    mid_now = (resid[...] + dot(attended, o_w[...])).astype(BF16)
    mid[...] = mid_now.reshape(band, width, channels)

    near = rows + 1
    mid_sibling = remote(
        mid.at[pl.ds(other * (rows - 1), near)],
        midx.at[core, pl.ds(core, near)],
        c_send.at[0],
        c_recv.at[0],
        sibling,
    )
    mid_down = remote(
        mid.at[pl.ds(band - 1, 1)],
        midx.at[core, pl.ds(0, 1)],
        c_send.at[1],
        c_recv.at[1 + core],
        2 * chip + 2,
    )
    mid_up = remote(
        mid.at[pl.ds(0, 1)],
        midx.at[core, pl.ds(rows + 1, 1)],
        c_send.at[2],
        c_recv.at[1 + core],
        2 * chip - 1,
    )

    @pl.when(has_next)
    def _():
        mid_down.start()

    @pl.when(has_prev)
    def _():
        mid_up.start()

    mid_sibling.start()
    midx[core, pl.ds(1 - core, near)] = mid[pl.ds(core * (rows - 1), near)]
    has_halo = ((core == 0) & has_prev) | ((core == 1) & has_next)
    edge_row = (rows + 1) * core

    @pl.when(jnp.logical_not(has_halo))
    def _():
        midx[:, pl.ds(edge_row, 1)] = jnp.zeros((2, 1, width, channels), BF16)

    own[...] = activate(stk[2:4].reshape(2 * rows * width, channels)).reshape(own.shape)
    cache_out = pltpu.make_async_copy(own, next_cache, w_sem.at[10])
    cache_out.start()

    for copy in to_sibling:
        copy.wait_send()

    @pl.when(has_prev)
    def _():
        pass_above.wait_send()

    @pl.when(has_next)
    def _():
        pass_below.wait_send()

    @pl.when(sends_down)
    def _():
        for copy in down_halo:
            copy.wait_send()

    @pl.when(sends_up)
    def _():
        for copy in up_halo:
            copy.wait_send()

    def sent(block, carry):
        whole = keys.at[block * ny + y]

        @pl.when((block <= z) & (z < nz - 1))
        def _():
            remote(whole, whole, z_send.at[block], z_recv.at[0, 0], sibling).wait_send()

        @pl.when((block >= z) & (z > 0))
        def _():
            remote(whole, whole, z_send.at[nz + block], z_recv.at[0, 0], sibling).wait_send()

        if ny > 1:
            remote(whole, whole, y_send.at[block], y_recv.at[0], sibling).wait_send()
        return carry

    lax.fori_loop(0, nz, sent, 0)

    remote(
        midx.at[other, pl.ds(1 - core, near)],
        midx.at[other, pl.ds(1 - core, near)],
        c_send.at[0],
        c_recv.at[0],
        sibling,
    ).wait_recv()

    @pl.when(has_halo)
    def _():
        for f in range(2):
            landed = midx.at[f, pl.ds(edge_row, 1)]
            remote(landed, landed, c_send.at[0], c_recv.at[1 + f], sibling).wait_recv()

    for f in range(2):
        mid3[f] = with_columns(midx[f].reshape((rows + 2) * width, channels), width)

    fine = 2 * width
    at_row = lax.broadcasted_iota(jnp.int32, (fine, fine), 0)
    at_col = lax.broadcasted_iota(jnp.int32, (fine, fine), 1)
    weave = (at_col == (at_row % 2) * width + at_row // 2).astype(F32).astype(BF16)
    for a in range(2):
        sides = []
        for b in range(2):
            result = None
            for t in range(2):
                window = mid3[
                    :, (a + t) * width : (a + t + rows) * width,
                    b * channels : (b + 2) * channels,
                ].reshape(2 * rows * width, 2 * channels)
                term = dot_nt(window, up_p[a, b, t])
                result = term if result is None else result + term
            sides.append(result.astype(BF16).reshape(2, rows, width, outputs))
        for f in range(2):
            for r in range(rows):
                pair = jnp.concatenate([sides[0][f, r], sides[1][f, r]], axis=0)
                decoded[f, 2 * r + a] = lax.dot_general(
                    pair, weave, (((0,), (1,)), ((), ())), preferred_element_type=F32
                ).astype(BF16)

    cache_out.wait()
    mid_sibling.wait_send()

    @pl.when(has_next)
    def _():
        mid_down.wait_send()

    @pl.when(has_prev)
    def _():
        mid_up.wait_send()


def finish(decoded_in, cache_in, decoded, next_cache):
    decoded[...] = decoded_in[...]
    next_cache[...] = cache_in[...]


def solution(mesh):
    ny = 4 // mesh.shape["videos"]
    nz = mesh.shape["rows"] // (2 * ny)

    def shards(
        latents, conv_cache, norm_gain, conv_weight, attn_gain,
        query_weight, key_weight, value_weight, out_weight, up_weight,
    ):
        frames, rows, width, channels = latents.shape
        outputs = up_weight.shape[3]
        band = 2 * rows
        vmem = pl.BlockSpec(memory_space=pltpu.VMEM)
        hbm = pl.BlockSpec(memory_space=pltpu.HBM)
        square = pltpu.VMEM((channels, channels), BF16)
        dma = pltpu.SemaphoreType.DMA
        decoded, next_cache = pl.pallas_call(
            functools.partial(kernel, nz, ny),
            out_shape=(
                jax.ShapeDtypeStruct((frames, 2 * rows, outputs, 2 * width), BF16),
                jax.ShapeDtypeStruct(latents.shape, BF16),
            ),
            in_specs=[hbm] * 2 + [vmem] * 2 + [hbm] * 6,
            out_specs=(vmem, hbm),
            scratch_shapes=[
                pltpu.VMEM((9, 3 * channels, channels), BF16),
                square, square, square, square,
                pltpu.VMEM((3, 3, outputs, channels), BF16),
                pltpu.VMEM((2, 2, 2, outputs, 2 * channels), BF16),
                pltpu.VMEM((4, rows, width, channels), BF16),
                pltpu.VMEM(latents.shape, BF16),
                pltpu.VMEM((3, band + 2, width, channels), BF16),
                pltpu.VMEM((3, (band + 2) * width, 3 * channels), BF16),
                pltpu.VMEM((band * width, channels), F32),
                pltpu.VMEM((nz * ny, band * width, channels), BF16),
                pltpu.VMEM((band * width, channels), BF16),
                pltpu.VMEM((band * width, 1), F32),
                pltpu.VMEM((band * width, 1), F32),
                pltpu.VMEM((band * width, channels), F32),
                pltpu.VMEM((band, width, channels), BF16),
                pltpu.VMEM((2, rows + 2, width, channels), BF16),
                pltpu.VMEM((2, (rows + 2) * width, 3 * channels), BF16),
                dma((11,)), dma((6,)), dma((6,)),
                dma((2 * nz,)), dma((nz, band)), dma((nz,)), dma((nz,)),
                dma((3,)), dma((3,)),
            ],
            compiler_params=pltpu.CompilerParams(
                collective_id=0, has_side_effects=True, vmem_limit_bytes=60 * 1024 * 1024
            ),
        )(
            latents, conv_cache,
            norm_gain, attn_gain,
            conv_weight.reshape(9, 3 * channels, channels),
            query_weight, key_weight, value_weight, out_weight, up_weight.swapaxes(2, 3),
        )
        decoded, next_cache = pl.pallas_call(
            finish,
            out_shape=(
                jax.ShapeDtypeStruct(decoded.shape, BF16),
                jax.ShapeDtypeStruct(next_cache.shape, BF16),
            ),
            in_specs=[vmem] * 2,
            out_specs=(vmem, vmem),
        )(decoded, next_cache)
        return decoded.swapaxes(2, 3), next_cache

    split = P("videos", "rows", None, None)
    return jax.shard_map(
        shards,
        mesh=mesh,
        in_specs=(split, split) + (P(),) * 8,
        out_specs=(split, split),
        check_vma=False,
    )
```
